32 devices in a mesh: group: 2 (over y), user: 2 (over core), cand: 8 (over z, x).
Axes of the slice: x: 2, y: 2, z: 4, core: 2. Of those that a mesh axis runs over, the one named last changes fastest.
Arguments:
- history: bfloat16 [4, 1024, 1024], P(('group', 'user'), None, 'cand'), parts along dimension 0, may hold values from -6 to 6
- hist_len: int32 [4], P(('group', 'user')), parts along dimension 0, may hold values from 256 to 1024
- tile_counts: int32 [4, 8], P(('group', 'user'), 'cand'), parts along dimension 0, may hold values from 0 to 3, as said below
- cand_emb: bfloat16 [4, 3072, 1024], P(('group', 'user'), 'cand'), parts along dimension 0, may hold values from -3 to 3
- w_in: bfloat16 [1024, 4096], P(None, 'cand'), may hold values from -1 to 1
- out_gain: float32 [1024], replicated, may hold values from 0.25 to 1.75
- w_out: bfloat16 [1024, 1024], P(None, 'cand'), may hold values from -0.1875 to 0.1875
Outputs:
- cand_out: bfloat16 [4, 3072, 1024], P(('group', 'user'), 'cand'), parts along dimension 0
The draws below stay inside these ranges and needn't reach their ends.
There are 2 independent parts, one for each index of `group`. The reference program is written for one: setup_inputs(seed, part) draws one part's arguments, and reference() takes and returns one part's arrays. A program takes and returns all parts, laid end to end along the dimension named above; an argument that names none is the same for every part. Nothing has to cross between parts.
Inputs may be any that keep to these rules, and one draw needn't show every extreme that they name: In each user's row of tile_counts exactly 1 entries equal 3, 2 * (1) entries are 0 and all others are 1, so that each row sums to its number of entries; which entries take which value is random.
All inputs are finite; a program needn't handle non-finite values.
Results may differ from the reference program's by a relative error of at most 0.0069.
Values may be sent and summed in bfloat16 or wider, within the bound.
A program may use at most 64 MiB of HBM per device.

```python
import math
import jax
import jax.numpy as jnp
from jax import lax

D = 1024
HEADS = 8
DH = 128
HIST = 1024
TILE = 128
CAP = 3
USERS = 2
SLOTS = 3072
N_CAND = 8


def draw_tile_counts(key, part):
    row_keys = jax.random.split(key, USERS)
    heavy = N_CAND // 8
    index_row = jnp.arange(N_CAND, dtype=jnp.int32)
    pattern = jnp.where(index_row < heavy, CAP, jnp.where(index_row < CAP * heavy, 0, 1)).astype(jnp.int32)

    def one_row(row_key):
        order = jax.random.permutation(row_key, N_CAND)
        return jnp.take(pattern, order)
    return jax.vmap(one_row)(row_keys).astype(jnp.int32)


def unit_entries(key, shape):
    return jnp.clip(jax.random.normal(key, shape, jnp.float32), -6.0, 6.0)


def draw_w_in(key, part):
    base_key = jax.random.fold_in(key, 11)
    extra_key = jax.random.fold_in(key, 12)
    mix_key = jax.random.fold_in(key, 13)
    base = unit_entries(base_key, (D, 4 * D))
    extra = unit_entries(extra_key, (D, D))
    head_mix = jax.random.uniform(mix_key, (HEADS,), jnp.float32, 0.6, 0.9)
    column_mix = jnp.repeat(head_mix, DH)[None, :]
    query_part = base[:, 2 * D:3 * D]
    key_part = column_mix * query_part + jnp.sqrt(1.0 - column_mix * column_mix) * extra
    whole = jnp.concatenate([base[:, :3 * D], key_part], axis=1) * D ** (-0.5)
    return jnp.clip(whole, -1.0, 1.0).astype(jnp.bfloat16)


def level_of(own_key, dims, cuts, least, top_value):
    level = 1.0
    for position, blocks in cuts:
        steps = jax.random.uniform(jax.random.fold_in(jax.random.fold_in(own_key, 6), position), (blocks,), jnp.float32, least / len(cuts), top_value / len(cuts))
        level = level * jnp.repeat(jnp.exp(steps), dims[position] // blocks).reshape((-1,) + (1,) * (len(dims) - 1 - position))
    return level


def gaussian(stream_key, extent, scale, most, shards=(), kind=jnp.bfloat16):
    drawn = scale * jax.random.normal(stream_key, extent, jnp.float32)
    if shards:
        drawn = drawn * level_of(stream_key, extent, shards, -0.22, 0.18)
    return jnp.clip(drawn, -most, most).astype(kind)


def setup_inputs(seed: int = 0, part: int = 0) -> dict:
    streams_of = jax.random.split(jax.random.key(seed), 8)
    part_splits = jax.random.split(jax.random.fold_in(streams_of[7], part), 8)
    return {
        "history": gaussian(part_splits[0], (USERS, HIST, D), 1.0, 6.0, ((0, 2), (2, 8))),
        "hist_len": jax.random.randint(part_splits[1], (USERS,), HIST // 4, HIST + 1).astype(jnp.int32),
        "tile_counts": draw_tile_counts(jax.random.fold_in(jax.random.fold_in(streams_of[7], part), 71), part),
        "cand_emb": gaussian(part_splits[3], (USERS, SLOTS, D), 0.5, 3.0, ((0, 2), (1, 8))),
        "w_in": draw_w_in(jax.random.fold_in(streams_of[7], 71), part),
        "out_gain": jnp.clip(1.0 + 0.15 * jax.random.normal(streams_of[5], (D,), jnp.float32), 0.25, 1.75),
        "w_out": gaussian(streams_of[6], (D, D), D ** -0.5, 0.1875, ((1, 8),)),
    }


def layer_norm(values):
    center = values - lax.optimization_barrier(jnp.mean(values, axis=-1, keepdims=True))
    spread = lax.optimization_barrier(jnp.mean(center * center, axis=-1, keepdims=True))
    return center * lax.rsqrt(spread + 1e-05)

def reference(history, hist_len, tile_counts, cand_emb, w_in, out_gain, w_out):
    score_scale = 1.0 / math.sqrt(DH)
    kv_weights = jnp.concatenate([w_in[:, D:2 * D], w_in[:, 3 * D:]], axis=1)
    results = []
    for user_row in range(USERS):
        hist_normed = layer_norm(history[user_row].astype(jnp.float32)).astype(jnp.bfloat16)
        hist_kv = jax.nn.silu(jnp.dot(hist_normed, kv_weights, preferred_element_type=jnp.float32)).astype(jnp.bfloat16)
        hist_values = hist_kv[:, :D].reshape(HIST, HEADS, DH).astype(jnp.float32)
        hist_keys = hist_kv[:, D:].reshape(HIST, HEADS, DH).astype(jnp.float32)
        keep_keys = jnp.arange(HIST, dtype=jnp.int32) < hist_len[user_row]
        emb_blocks = cand_emb[user_row].reshape(N_CAND, CAP * TILE, D)

        def score_block(block_args):
            embedded, block_count = block_args
            normed = layer_norm(embedded.astype(jnp.float32)).astype(jnp.bfloat16)
            proj = jax.nn.silu(jnp.dot(normed, w_in, preferred_element_type=jnp.float32)).astype(jnp.bfloat16)
            rows_here = proj.shape[0]
            gate_part = proj[:, :D].astype(jnp.float32)
            cand_values = proj[:, D:2 * D].reshape(rows_here, HEADS, DH).astype(jnp.float32)
            queries = proj[:, 2 * D:3 * D].reshape(rows_here, HEADS, DH).astype(jnp.float32)
            cand_keys = proj[:, 3 * D:].reshape(rows_here, HEADS, DH).astype(jnp.float32)
            scores = jnp.einsum('rhe,the->hrt', queries, hist_keys) * score_scale
            attn_weights = jnp.where(keep_keys[None, None, :], jax.nn.silu(scores), 0.0).astype(jnp.bfloat16)
            attn = jnp.einsum('hrt,the->rhe', attn_weights.astype(jnp.float32), hist_values)
            own_score = jax.nn.silu(lax.optimization_barrier(jnp.sum(queries * cand_keys, axis=-1)) * score_scale)
            attn = (attn + own_score[:, :, None] * cand_values).reshape(rows_here, D)
            gated = (layer_norm(attn) * out_gain[None, :] * gate_part).astype(jnp.bfloat16)
            output = embedded.astype(jnp.float32) + jnp.dot(gated, w_out, preferred_element_type=jnp.float32)
            live = jnp.arange(rows_here, dtype=jnp.int32) < block_count * TILE
            return jnp.where(live[:, None], output, 0.0).astype(jnp.bfloat16)
        scored = lax.map(score_block, (emb_blocks, tile_counts[user_row]))
        results.append(scored.reshape(SLOTS, D))
    return jnp.stack(results)
```

```python
import functools
import math

import jax
import jax.numpy as jnp
from jax import lax
from jax.experimental import pallas as pl
from jax.experimental.pallas import tpu as pltpu
from jax.sharding import PartitionSpec as P

D = 1024
HEADS = 8
DH = 128
TILE = 128
RING = 8
MESH = pl.DeviceIdType.MESH


def layer_norm(values):
    center = values - jnp.mean(values, axis=-1, keepdims=True)
    spread = jnp.mean(center * center, axis=-1, keepdims=True)
    return center * lax.rsqrt(spread + 1e-05)


def half_silu(half):
    return half + half * jnp.tanh(half)


def cand_of(place):
    high = place // 4
    return (1 - high) * (2 * place) + high * (15 - 2 * place)


def place_of(cand):
    row, column = cand // 2, cand % 2
    return (1 - column) * row + column * (7 - row)


def fused_kernel(
    length_ref, count_ref, hist_ref, w_ref, wo_ref, cand_ref, gain_ref, out_ref,
    hb, wb, ob, nb, hn, pb, kvb, ab, gb,
    ring_send, ring_recv, side_send, side_recv, local_sem,
):
    group = lax.axis_index("group")
    user = lax.axis_index("user")
    me = lax.axis_index("cand")
    place = place_of(me)
    slots = cand_ref.shape[1]
    events = hist_ref.shape[1]

    def shard_at(offset):
        return cand_of((place + offset + RING) % RING)

    core_peer = {"user": 1 - user}
    y_peer = {"group": 1 - group}
    ring_peer = ({"cand": shard_at(1)}, {"cand": shard_at(-1)})
    started = []

    quarter = D // 4
    half = D // 2
    w_start = (2 * group + user) * quarter
    w_core = (2 * group + 1 - user) * quarter
    w_y = (2 * (1 - group) + user) * quarter
    w_diag = (2 * (1 - group) + 1 - user) * quarter
    o_start = user * half
    o_core = (1 - user) * half
    kinds = (
        (w_ref, wb, w_start, quarter),
        (hist_ref.at[0], hb, 0, events),
        (wo_ref, ob, o_start, half),
    )

    barrier = pltpu.get_barrier_semaphore()
    for peer in (ring_peer[0], ring_peer[1], core_peer, y_peer):
        pl.semaphore_signal(barrier, inc=1, device_id=peer, device_id_type=MESH)
    pl.semaphore_wait(barrier, 4)

    def ring_copy(kind, way, step, shard, first):
        source, buffer, start, size = kinds[kind]
        if step == 3:
            size = size // 2
            start = start + way * size
        rows = pl.ds(pl.multiple_of(start, 64), size)
        spot = buffer.at[shard, rows, :]
        return pltpu.make_async_remote_copy(
            src_ref=source.at[rows, :] if first else spot,
            dst_ref=spot,
            send_sem=ring_send.at[kind, way, step],
            recv_sem=ring_recv.at[kind, way, step],
            device_id=ring_peer[way],
            device_id_type=MESH,
        )

    def ring_start(kind, step):
        for way in range(2):
            shard = shard_at(-step if way == 0 else step)
            copy = ring_copy(kind, way, step, shard, step == 0)
            copy.start()
            started.append(copy)

    def ring_wait(kind, step):
        for way in range(2):
            shard = shard_at(-1 - step if way == 0 else step + 1)
            ring_copy(kind, way, step, shard, False).wait_recv()

    def spots(step):
        return ((6, 4),) if step == 3 else ((2 * step, -1 - step), (2 * step + 1, step + 1))

    def side_copy(kind, index, offset):
        buffer, start, size, peer = (
            (wb, w_start, quarter, core_peer),
            (wb, w_start, quarter, y_peer),
            (wb, w_y, quarter, core_peer),
            (ob, o_start, half, core_peer),
        )[kind]
        spot = buffer.at[shard_at(offset), pl.ds(pl.multiple_of(start, 256), size), :]
        return pltpu.make_async_remote_copy(
            src_ref=spot, dst_ref=spot,
            send_sem=side_send.at[kind, index], recv_sem=side_recv.at[kind, index],
            device_id=peer, device_id_type=MESH,
        )

    def side_start(kind, step):
        for index, offset in spots(step):
            copy = side_copy(kind, index, offset)
            copy.start()
            started.append(copy)

    def side_wait(kind, step):
        for index, offset in spots(step):
            buffer, start, size, peer = (
                (wb, w_core, quarter, core_peer),
                (wb, w_y, quarter, y_peer),
                (wb, w_diag, quarter, core_peer),
                (ob, o_core, half, core_peer),
            )[kind]
            spot = buffer.at[shard_at(offset), pl.ds(pl.multiple_of(start, 256), size), :]
            pltpu.make_async_remote_copy(
                src_ref=spot, dst_ref=spot,
                send_sem=side_send.at[kind, index], recv_sem=side_recv.at[kind, index],
                device_id=peer, device_id_type=MESH,
            ).wait_recv()

    W, H, O = 0, 1, 2
    CORE, Y, DIAG, OCORE = 0, 1, 2, 3

    ring_start(W, 0)
    ring_start(H, 0)
    own = [
        pltpu.make_async_copy(w_ref, wb.at[me], local_sem.at[0]),
        pltpu.make_async_copy(hist_ref.at[0], hb.at[me], local_sem.at[1]),
        pltpu.make_async_copy(wo_ref, ob.at[me], local_sem.at[2]),
    ]
    for copy in own:
        copy.start()
    nb[...] = layer_norm(cand_ref[0].astype(jnp.float32)).astype(jnp.bfloat16)
    for copy in own:
        copy.wait()

    def project_cand(shard):
        product = jnp.dot(nb[...], wb[shard], preferred_element_type=jnp.float32)
        act = half_silu(0.5 * product).astype(jnp.bfloat16)
        for i in range(4):
            pb[4 * shard + i] = act[:, i * DH : (i + 1) * DH]

    def project_pair(step):
        @pl.loop(0, 2)
        def _(way):
            project_cand(shard_at((1 - 2 * way) * (step + 1)))

    project_cand(me)
    for step in range(4):
        ring_wait(W, step)
        if step < 3:
            ring_start(W, step + 1)
        side_start(Y, step)
        side_start(CORE, step)
        ring_wait(H, step)
        if step < 3:
            ring_start(H, step + 1)
        if step >= 1:
            ring_wait(O, step - 1)
        ring_start(O, step)
        if step >= 1:
            side_start(OCORE, step - 1)
            side_wait(Y, step - 1)
            side_start(DIAG, step - 1)
            side_wait(CORE, step - 1)
            side_wait(DIAG, step - 1)
            if step < 3:
                project_pair(step - 1)

    chunk = 128

    @pl.loop(0, events // chunk)
    def _(i):
        rows = pl.ds(pl.multiple_of(i * chunk, chunk), chunk)
        whole = jnp.concatenate([hb[c, rows, :] for c in range(RING)], axis=1)
        hn[rows, :] = layer_norm(whole.astype(jnp.float32)).astype(jnp.bfloat16)

    length = length_ref[0]
    block = 256

    def project_hist(shard):
        @pl.when((shard % 4) // 2 == 1)
        def _():
            first = 4 * shard - 8 - 8 * (shard // 4)

            @pl.loop(0, events // block)
            def _(i):
                start = pl.multiple_of(i * block, block)
                rows = pl.ds(start, block)
                product = jnp.dot(hn[rows, :], wb[shard], preferred_element_type=jnp.float32)
                act = half_silu(0.5 * product)
                event = lax.broadcasted_iota(jnp.int32, act.shape, 0) + start
                act = jnp.where(event < length, act, 0.0).astype(jnp.bfloat16)
                for j in range(4):
                    kvb[first + j, rows, :] = act[:, j * DH : (j + 1) * DH]

    @pl.loop(-2, 3)
    def _(offset):
        project_hist(shard_at(offset))

    project_pair(2)
    project_hist(shard_at(3))
    project_hist(shard_at(-3))
    ring_wait(O, 3)
    side_start(OCORE, 3)
    side_wait(Y, 3)
    side_start(DIAG, 3)
    side_wait(CORE, 3)
    side_wait(DIAG, 3)
    project_cand(shard_at(4))
    project_hist(shard_at(4))

    half_scale = 0.5 / math.sqrt(DH)

    @pl.loop(0, HEADS)
    def _(head):
        query = pb[2 * HEADS + head]
        scores = lax.dot_general(
            query, kvb[HEADS + head], (((1,), (1,)), ((), ())),
            preferred_element_type=jnp.float32,
        )
        weights = half_silu(scores * half_scale).astype(jnp.bfloat16)
        mixed = jnp.dot(weights, kvb[head], preferred_element_type=jnp.float32)
        own_sum = jnp.sum(
            query.astype(jnp.float32) * pb[3 * HEADS + head].astype(jnp.float32),
            axis=-1, keepdims=True,
        )
        own_weight = half_silu(own_sum * half_scale)
        ab[head] = mixed + own_weight * pb[HEADS + head].astype(jnp.float32)

    for step in range(4):
        side_wait(OCORE, step)

    count = count_ref[0, 0]

    @pl.loop(0, slots // chunk)
    def _(i):
        start = pl.multiple_of(i * chunk, chunk)
        rows = pl.ds(start, chunk)
        attn = jnp.concatenate([ab[h, rows, :] for h in range(HEADS)], axis=1)
        gate = jnp.concatenate([pb[h, rows, :] for h in range(HEADS)], axis=1)
        gb[rows, :] = (layer_norm(attn) * gain_ref[...] * gate.astype(jnp.float32)).astype(
            jnp.bfloat16
        )

    for j in range(4):
        columns = pl.ds(j * 256, 256)
        pair = jnp.concatenate([ob[2 * j], ob[2 * j + 1]], axis=1)
        added = jnp.dot(gb[...], pair, preferred_element_type=jnp.float32)
        result = cand_ref[0, :, columns].astype(jnp.float32) + added
        slot = lax.broadcasted_iota(jnp.int32, result.shape, 0)
        out_ref[0, :, columns] = jnp.where(slot < count * TILE, result, 0.0).astype(jnp.bfloat16)

    for copy in started:
        copy.wait_send()


def fused_shards(history, hist_len, tile_counts, cand_emb, w_in, out_gain, w_out):
    slots = cand_emb.shape[1]
    events = history.shape[1]
    blocks = 4 * D // DH
    anywhere = pl.BlockSpec(memory_space=pl.ANY)
    vmem = pl.BlockSpec(memory_space=pltpu.VMEM)
    smem = pl.BlockSpec(memory_space=pltpu.SMEM)
    return pl.pallas_call(
        fused_kernel,
        out_shape=jax.ShapeDtypeStruct(cand_emb.shape, jnp.bfloat16),
        in_specs=[smem, smem, anywhere, anywhere, anywhere, vmem, vmem],
        out_specs=vmem,
        scratch_shapes=[
            pltpu.VMEM((RING, events, D // RING), jnp.bfloat16),
            pltpu.VMEM((RING, D, 4 * D // RING), jnp.bfloat16),
            pltpu.VMEM((RING, D, D // RING), jnp.bfloat16),
            pltpu.VMEM((slots, D), jnp.bfloat16),
            pltpu.VMEM((events, D), jnp.bfloat16),
            pltpu.VMEM((blocks, slots, DH), jnp.bfloat16),
            pltpu.VMEM((blocks // 2, events, DH), jnp.bfloat16),
            pltpu.VMEM((HEADS, slots, DH), jnp.float32),
            pltpu.VMEM((slots, D), jnp.bfloat16),
            pltpu.SemaphoreType.DMA((3, 2, 4)),
            pltpu.SemaphoreType.DMA((3, 2, 4)),
            pltpu.SemaphoreType.DMA((4, 7)),
            pltpu.SemaphoreType.DMA((4, 7)),
            pltpu.SemaphoreType.DMA((3,)),
        ],
        compiler_params=pltpu.CompilerParams(
            collective_id=0, has_side_effects=True, vmem_limit_bytes=56 * 1024 * 1024
        ),
        name="score_fused",
    )(hist_len, tile_counts, history, w_in, w_out, cand_emb, out_gain.reshape(1, D))


def attend_rows(carry, kv_piece, queries, length, score_scale):
    key_count = kv_piece.shape[0]
    values = kv_piece[:, :D].reshape(key_count, HEADS, DH)
    key_heads = kv_piece[:, D:].reshape(key_count, HEADS, DH)
    scores = (
        jnp.einsum("rhe,the->hrt", queries, key_heads, preferred_element_type=jnp.float32)
        * score_scale
    )
    positions = jnp.arange(key_count, dtype=jnp.int32)
    weights = jnp.where(positions[None, None, :] < length, jax.nn.silu(scores), 0.0).astype(
        jnp.bfloat16
    )
    mixed_sum = jnp.einsum("hrt,the->rhe", weights, values, preferred_element_type=jnp.float32)
    return mixed_sum.reshape(carry.shape)


def score_rows(embedded, history, length, w_in, out_gain, w_out):
    score_scale = 1.0 / math.sqrt(DH)
    rows_here = embedded.shape[0]
    normed = layer_norm(embedded.astype(jnp.float32)).astype(jnp.bfloat16)
    initial = jnp.zeros((rows_here, D), jnp.float32)
    own_events = lax.all_to_all(history, "cand", split_axis=0, concat_axis=1, tiled=True)
    hist_normed = layer_norm(own_events.astype(jnp.float32)).astype(jnp.bfloat16)
    stacked = jnp.concatenate([normed, hist_normed], axis=0)
    projected = jax.nn.silu(
        jnp.dot(
            stacked,
            lax.all_gather(w_in, "cand", axis=1, tiled=True),
            preferred_element_type=jnp.float32,
        )
    ).astype(jnp.bfloat16)
    proj_rows = projected[:rows_here]
    hist_proj = projected[rows_here:]
    kv_local = jnp.concatenate([hist_proj[:, D : 2 * D], hist_proj[:, 3 * D :]], axis=1)
    queries = proj_rows[:, 2 * D : 3 * D].reshape(rows_here, HEADS, DH)
    summed = attend_rows(
        initial, lax.all_gather(kv_local, "cand", axis=0, tiled=True), queries, length, score_scale
    )
    gate_part = proj_rows[:, :D].astype(jnp.float32)
    cand_values = proj_rows[:, D : 2 * D].reshape(rows_here, HEADS, DH).astype(jnp.float32)
    cand_keys = proj_rows[:, 3 * D :].reshape(rows_here, HEADS, DH).astype(jnp.float32)
    own_score = jax.nn.silu(jnp.sum(queries.astype(jnp.float32) * cand_keys, axis=-1) * score_scale)
    attn = summed + (own_score[:, :, None] * cand_values).reshape(rows_here, D)
    gated = (layer_norm(attn) * out_gain[None, :] * gate_part).astype(jnp.bfloat16)
    residual = embedded.astype(jnp.float32)
    return (
        residual
        + jnp.dot(
            gated,
            lax.all_gather(w_out, "cand", axis=1, tiled=True),
            preferred_element_type=jnp.float32,
        )
    ).astype(jnp.bfloat16)


def shards(history, hist_len, tile_counts, cand_emb, w_in, out_gain, w_out):
    tile_total = tile_counts[0, 0]
    length = hist_len[0]
    slot_rows = cand_emb[0]
    slot_count = slot_rows.shape[0]
    own_history = history[0]
    scored = score_rows(slot_rows, own_history, length, w_in, out_gain, w_out)
    live = jnp.arange(slot_count, dtype=jnp.int32) < tile_total * TILE
    result = jnp.where(live[:, None], scored, jnp.zeros_like(scored))
    return result[None]


def solution(mesh):
    in_specs = (
        P(("group", "user"), None, "cand"),
        P(("group", "user")),
        P(("group", "user"), "cand"),
        P(("group", "user"), "cand", None),
        P(None, "cand"),
        P(),
        P(None, "cand"),
    )
    out_specs = P(("group", "user"), "cand", None)
    sizes = tuple(mesh.shape[name] for name in ("group", "user", "cand"))
    body = fused_shards if sizes == (2, 2, RING) else shards
    return jax.shard_map(body, mesh=mesh, in_specs=in_specs, out_specs=out_specs, check_vma=False)
```

```python
import functools
import math

import jax
import jax.numpy as jnp
from jax import lax
from jax.experimental import pallas as pl
from jax.experimental.pallas import tpu as pltpu
from jax.sharding import PartitionSpec as P

D = 1024
HEADS = 8
DH = 128
TILE = 128
RING = 8
MESH = pl.DeviceIdType.MESH


def layer_norm(values):
    center = values - jnp.mean(values, axis=-1, keepdims=True)
    spread = jnp.mean(center * center, axis=-1, keepdims=True)
    return center * lax.rsqrt(spread + 1e-05)


def half_silu(half):
    return half + half * jnp.tanh(half)


def cand_of(place):
    high = place // 4
    return (1 - high) * (2 * place) + high * (15 - 2 * place)


def place_of(cand):
    row, column = cand // 2, cand % 2
    return (1 - column) * row + column * (7 - row)


def fused_kernel(
    length_ref, hist_ref, w_ref, wo_ref, cand_ref, gain_ref, out_ref,
    hb, wb, ob, nb, hn, pb, kvb, ab, gb,
    ring_send, ring_recv, side_send, side_recv, local_sem,
):
    group = lax.axis_index("group")
    user = lax.axis_index("user")
    me = lax.axis_index("cand")
    place = place_of(me)
    slots = cand_ref.shape[1]
    events = hist_ref.shape[1]

    def shard_at(offset):
        return cand_of((place + offset + RING) % RING)

    core_peer = {"user": 1 - user}
    y_peer = {"group": 1 - group}
    ring_peer = ({"cand": shard_at(1)}, {"cand": shard_at(-1)})
    started = []

    quarter = D // 4
    half = D // 2
    w_start = (2 * group + user) * quarter
    w_core = (2 * group + 1 - user) * quarter
    w_y = (2 * (1 - group) + user) * quarter
    w_diag = (2 * (1 - group) + 1 - user) * quarter
    o_start = user * half
    o_core = (1 - user) * half
    kinds = (
        (w_ref, wb, w_start, quarter),
        (hist_ref.at[0], hb, 0, events),
        (wo_ref, ob, o_start, half),
    )

    barrier = pltpu.get_barrier_semaphore()
    for peer in (ring_peer[0], ring_peer[1], core_peer, y_peer):
        pl.semaphore_signal(barrier, inc=1, device_id=peer, device_id_type=MESH)
    pl.semaphore_wait(barrier, 4)

    def ring_copy(kind, way, step, shard, first):
        source, buffer, start, size = kinds[kind]
        if step == 3:
            size = size // 2
            start = start + way * size
        rows = pl.ds(pl.multiple_of(start, 64), size)
        spot = buffer.at[shard, rows, :]
        return pltpu.make_async_remote_copy(
            src_ref=source.at[rows, :] if first else spot,
            dst_ref=spot,
            send_sem=ring_send.at[kind, way, step],
            recv_sem=ring_recv.at[kind, way, step],
            device_id=ring_peer[way],
            device_id_type=MESH,
        )

    def ring_start(kind, step):
        for way in range(2):
            shard = shard_at(-step if way == 0 else step)
            copy = ring_copy(kind, way, step, shard, step == 0)
            copy.start()
            started.append(copy)

    def ring_wait(kind, step):
        for way in range(2):
            shard = shard_at(-1 - step if way == 0 else step + 1)
            ring_copy(kind, way, step, shard, False).wait_recv()

    def spots(step):
        return ((6, 4),) if step == 3 else ((2 * step, -1 - step), (2 * step + 1, step + 1))

    def side_copy(kind, index, offset):
        buffer, start, size, peer = (
            (wb, w_start, quarter, core_peer),
            (wb, w_start, quarter, y_peer),
            (wb, w_y, quarter, core_peer),
            (ob, o_start, half, core_peer),
        )[kind]
        spot = buffer.at[shard_at(offset), pl.ds(pl.multiple_of(start, 256), size), :]
        return pltpu.make_async_remote_copy(
            src_ref=spot, dst_ref=spot,
            send_sem=side_send.at[kind, index], recv_sem=side_recv.at[kind, index],
            device_id=peer, device_id_type=MESH,
        )

    def side_start(kind, step):
        for index, offset in spots(step):
            copy = side_copy(kind, index, offset)
            copy.start()
            started.append(copy)

    def side_wait(kind, step):
        for index, offset in spots(step):
            buffer, start, size, peer = (
                (wb, w_core, quarter, core_peer),
                (wb, w_y, quarter, y_peer),
                (wb, w_diag, quarter, core_peer),
                (ob, o_core, half, core_peer),
            )[kind]
            spot = buffer.at[shard_at(offset), pl.ds(pl.multiple_of(start, 256), size), :]
            pltpu.make_async_remote_copy(
                src_ref=spot, dst_ref=spot,
                send_sem=side_send.at[kind, index], recv_sem=side_recv.at[kind, index],
                device_id=peer, device_id_type=MESH,
            ).wait_recv()

    W, H, O = 0, 1, 2
    CORE, Y, DIAG, OCORE = 0, 1, 2, 3

    ring_start(W, 0)
    ring_start(H, 0)
    own = [
        pltpu.make_async_copy(w_ref, wb.at[me], local_sem.at[0]),
        pltpu.make_async_copy(hist_ref.at[0], hb.at[me], local_sem.at[1]),
        pltpu.make_async_copy(wo_ref, ob.at[me], local_sem.at[2]),
    ]
    for copy in own:
        copy.start()
    nb[...] = layer_norm(cand_ref[0].astype(jnp.float32)).astype(jnp.bfloat16)
    for copy in own:
        copy.wait()

    def project_cand(shard):
        product = jnp.dot(nb[...], wb[shard], preferred_element_type=jnp.float32)
        act = half_silu(0.5 * product).astype(jnp.bfloat16)
        for i in range(4):
            pb[4 * shard + i] = act[:, i * DH : (i + 1) * DH]

    def project_pair(step):
        @pl.loop(0, 2)
        def _(way):
            project_cand(shard_at((1 - 2 * way) * (step + 1)))

    def spread_rows(step):
        ring_wait(W, step)
        if step < 3:
            ring_start(W, step + 1)
        side_start(Y, step)
        side_start(CORE, step)
        ring_wait(H, step)
        if step < 3:
            ring_start(H, step + 1)

    def spread_out(step):
        ring_wait(O, step)
        if step < 3:
            ring_start(O, step + 1)
        side_start(OCORE, step)

    def gather_rows(step):
        side_wait(Y, step)
        side_start(DIAG, step)
        side_wait(CORE, step)
        side_wait(DIAG, step)

    chunk = 128
    block = 512
    length = length_ref[0]

    def project_hist(shard):
        @pl.when((shard % 4) // 2 == 1)
        def _():
            first = 4 * shard - 8 - 8 * (shard // 4)

            @pl.loop(0, events // block)
            def _(i):
                start = pl.multiple_of(i * block, block)
                rows = pl.ds(start, block)
                product = jnp.dot(hn[rows, :], wb[shard], preferred_element_type=jnp.float32)
                act = half_silu(0.5 * product)
                event = lax.broadcasted_iota(jnp.int32, act.shape, 0) + start
                act = jnp.where(event < length, act, 0.0).astype(jnp.bfloat16)
                for j in range(4):
                    kvb[first + j, rows, :] = act[:, j * DH : (j + 1) * DH]

    half_scale = 0.5 / math.sqrt(DH)

    def attend(first):
        @pl.loop(0, HEADS // 2)
        def _(i):
            head = first + i
            query = pb[2 * HEADS + head]
            scores = lax.dot_general(
                query, kvb[HEADS + head], (((1,), (1,)), ((), ())),
                preferred_element_type=jnp.float32,
            )
            weights = half_silu(scores * half_scale).astype(jnp.bfloat16)
            mixed = jnp.dot(weights, kvb[head], preferred_element_type=jnp.float32)
            own_sum = jnp.sum(
                query.astype(jnp.float32) * pb[3 * HEADS + head].astype(jnp.float32),
                axis=-1, keepdims=True,
            )
            own_weight = half_silu(own_sum * half_scale)
            ab[head] = mixed + own_weight * pb[HEADS + head].astype(jnp.float32)

    project_cand(me)
    spread_rows(0)
    spread_rows(1)
    ring_start(O, 0)
    gather_rows(0)
    project_pair(0)
    spread_rows(2)
    spread_out(0)
    gather_rows(1)
    project_pair(1)
    spread_rows(3)
    spread_out(1)
    @pl.loop(0, events // chunk)
    def _(i):
        rows = pl.ds(pl.multiple_of(i * chunk, chunk), chunk)
        whole = jnp.concatenate([hb[c, rows, :] for c in range(RING)], axis=1)
        hn[rows, :] = layer_norm(whole.astype(jnp.float32)).astype(jnp.bfloat16)

    gather_rows(2)

    @pl.loop(-1, 2)
    def _(offset):
        project_hist(shard_at(offset))

    spread_out(2)

    @pl.loop(0, 2)
    def _(i):
        project_hist(shard_at(2 - 4 * i))

    project_pair(2)
    spread_out(3)
    side_wait(Y, 3)
    side_start(DIAG, 3)

    @pl.loop(0, 2)
    def _(i):
        project_hist(shard_at(3 - 6 * i))

    near = (HEADS // 2) * (me % 2)
    attend(near)
    side_wait(CORE, 3)
    side_wait(DIAG, 3)
    project_cand(shard_at(4))
    project_hist(shard_at(4))
    attend(HEADS // 2 - near)

    for step in range(4):
        side_wait(OCORE, step)

    @pl.loop(0, slots // chunk)
    def _(i):
        start = pl.multiple_of(i * chunk, chunk)
        rows = pl.ds(start, chunk)
        attn = jnp.concatenate([ab[h, rows, :] for h in range(HEADS)], axis=1)
        gate = jnp.concatenate([pb[h, rows, :] for h in range(HEADS)], axis=1)
        gb[rows, :] = (layer_norm(attn) * gain_ref[...] * gate.astype(jnp.float32)).astype(
            jnp.bfloat16
        )

    for j in range(4):
        columns = pl.ds(j * 256, 256)
        pair = jnp.concatenate([ob[2 * j], ob[2 * j + 1]], axis=1)
        added = jnp.dot(gb[...], pair, preferred_element_type=jnp.float32)
        result = cand_ref[0, :, columns].astype(jnp.float32) + added
        out_ref[0, :, columns] = result.astype(jnp.bfloat16)

    for copy in started:
        copy.wait_send()


def fused_shards(history, hist_len, tile_counts, cand_emb, w_in, out_gain, w_out):
    slots = cand_emb.shape[1]
    events = history.shape[1]
    blocks = 4 * D // DH
    anywhere = pl.BlockSpec(memory_space=pl.ANY)
    vmem = pl.BlockSpec(memory_space=pltpu.VMEM)
    smem = pl.BlockSpec(memory_space=pltpu.SMEM)
    scored = pl.pallas_call(
        fused_kernel,
        out_shape=jax.ShapeDtypeStruct(cand_emb.shape, jnp.bfloat16),
        in_specs=[smem, anywhere, anywhere, anywhere, vmem, vmem],
        out_specs=vmem,
        scratch_shapes=[
            pltpu.VMEM((RING, events, D // RING), jnp.bfloat16),
            pltpu.VMEM((RING, D, 4 * D // RING), jnp.bfloat16),
            pltpu.VMEM((RING, D, D // RING), jnp.bfloat16),
            pltpu.VMEM((slots, D), jnp.bfloat16),
            pltpu.VMEM((events, D), jnp.bfloat16),
            pltpu.VMEM((blocks, slots, DH), jnp.bfloat16),
            pltpu.VMEM((blocks // 2, events, DH), jnp.bfloat16),
            pltpu.VMEM((HEADS, slots, DH), jnp.float32),
            pltpu.VMEM((slots, D), jnp.bfloat16),
            pltpu.SemaphoreType.DMA((3, 2, 4)),
            pltpu.SemaphoreType.DMA((3, 2, 4)),
            pltpu.SemaphoreType.DMA((4, 7)),
            pltpu.SemaphoreType.DMA((4, 7)),
            pltpu.SemaphoreType.DMA((3,)),
        ],
        compiler_params=pltpu.CompilerParams(
            collective_id=0, has_side_effects=True, vmem_limit_bytes=56 * 1024 * 1024
        ),
        name="score_fused",
    )(hist_len, history, w_in, w_out, cand_emb, out_gain.reshape(1, D))
    live = jnp.arange(slots, dtype=jnp.int32) < tile_counts[0, 0] * TILE
    return jnp.where(live[None, :, None], scored, jnp.zeros_like(scored))


def attend_rows(carry, kv_piece, queries, length, score_scale):
    key_count = kv_piece.shape[0]
    values = kv_piece[:, :D].reshape(key_count, HEADS, DH)
    key_heads = kv_piece[:, D:].reshape(key_count, HEADS, DH)
    scores = (
        jnp.einsum("rhe,the->hrt", queries, key_heads, preferred_element_type=jnp.float32)
        * score_scale
    )
    positions = jnp.arange(key_count, dtype=jnp.int32)
    weights = jnp.where(positions[None, None, :] < length, jax.nn.silu(scores), 0.0).astype(
        jnp.bfloat16
    )
    mixed_sum = jnp.einsum("hrt,the->rhe", weights, values, preferred_element_type=jnp.float32)
    return mixed_sum.reshape(carry.shape)


def score_rows(embedded, history, length, w_in, out_gain, w_out):
    score_scale = 1.0 / math.sqrt(DH)
    rows_here = embedded.shape[0]
    normed = layer_norm(embedded.astype(jnp.float32)).astype(jnp.bfloat16)
    initial = jnp.zeros((rows_here, D), jnp.float32)
    own_events = lax.all_to_all(history, "cand", split_axis=0, concat_axis=1, tiled=True)
    hist_normed = layer_norm(own_events.astype(jnp.float32)).astype(jnp.bfloat16)
    stacked = jnp.concatenate([normed, hist_normed], axis=0)
    projected = jax.nn.silu(
        jnp.dot(
            stacked,
            lax.all_gather(w_in, "cand", axis=1, tiled=True),
            preferred_element_type=jnp.float32,
        )
    ).astype(jnp.bfloat16)
    proj_rows = projected[:rows_here]
    hist_proj = projected[rows_here:]
    kv_local = jnp.concatenate([hist_proj[:, D : 2 * D], hist_proj[:, 3 * D :]], axis=1)
    queries = proj_rows[:, 2 * D : 3 * D].reshape(rows_here, HEADS, DH)
    summed = attend_rows(
        initial, lax.all_gather(kv_local, "cand", axis=0, tiled=True), queries, length, score_scale
    )
    gate_part = proj_rows[:, :D].astype(jnp.float32)
    cand_values = proj_rows[:, D : 2 * D].reshape(rows_here, HEADS, DH).astype(jnp.float32)
    cand_keys = proj_rows[:, 3 * D :].reshape(rows_here, HEADS, DH).astype(jnp.float32)
    own_score = jax.nn.silu(jnp.sum(queries.astype(jnp.float32) * cand_keys, axis=-1) * score_scale)
    attn = summed + (own_score[:, :, None] * cand_values).reshape(rows_here, D)
    gated = (layer_norm(attn) * out_gain[None, :] * gate_part).astype(jnp.bfloat16)
    residual = embedded.astype(jnp.float32)
    return (
        residual
        + jnp.dot(
            gated,
            lax.all_gather(w_out, "cand", axis=1, tiled=True),
            preferred_element_type=jnp.float32,
        )
    ).astype(jnp.bfloat16)


def shards(history, hist_len, tile_counts, cand_emb, w_in, out_gain, w_out):
    tile_total = tile_counts[0, 0]
    length = hist_len[0]
    slot_rows = cand_emb[0]
    slot_count = slot_rows.shape[0]
    own_history = history[0]
    scored = score_rows(slot_rows, own_history, length, w_in, out_gain, w_out)
    live = jnp.arange(slot_count, dtype=jnp.int32) < tile_total * TILE
    result = jnp.where(live[:, None], scored, jnp.zeros_like(scored))
    return result[None]


def solution(mesh):
    in_specs = (
        P(("group", "user"), None, "cand"),
        P(("group", "user")),
        P(("group", "user"), "cand"),
        P(("group", "user"), "cand", None),
        P(None, "cand"),
        P(),
        P(None, "cand"),
    )
    out_specs = P(("group", "user"), "cand", None)
    sizes = tuple(mesh.shape[name] for name in ("group", "user", "cand"))
    body = fused_shards if sizes == (2, 2, RING) else shards
    return jax.shard_map(body, mesh=mesh, in_specs=in_specs, out_specs=out_specs, check_vma=False)
```

```python
import functools
import math

import jax
import jax.numpy as jnp
from jax import lax
from jax.experimental import pallas as pl
from jax.experimental.pallas import tpu as pltpu
from jax.sharding import PartitionSpec as P

D = 1024
HEADS = 8
DH = 128
TILE = 128
RING = 8
MESH = pl.DeviceIdType.MESH


def layer_norm(values):
    center = values - jnp.mean(values, axis=-1, keepdims=True)
    spread = jnp.mean(center * center, axis=-1, keepdims=True)
    return center * lax.rsqrt(spread + 1e-05)


def half_silu(half):
    return half + half * jnp.tanh(half)


def cand_of(place):
    high = place // 4
    return (1 - high) * (2 * place) + high * (15 - 2 * place)


def place_of(cand):
    row, column = cand // 2, cand % 2
    return (1 - column) * row + column * (7 - row)


def fused_kernel(
    length_ref, hist_ref, w_ref, wo_ref, cand_ref, gain_ref, out_ref,
    hb, wb, ob, nb, hn, pb, kvb, ab, gb,
    ring_send, ring_recv, side_send, side_recv, local_sem,
):
    group = lax.axis_index("group")
    user = lax.axis_index("user")
    me = lax.axis_index("cand")
    place = place_of(me)
    slots = cand_ref.shape[1]
    events = hist_ref.shape[1]

    def shard_at(offset):
        return cand_of((place + offset + RING) % RING)

    core_peer = {"user": 1 - user}
    y_peer = {"group": 1 - group}
    ring_peer = ({"cand": shard_at(1)}, {"cand": shard_at(-1)})
    started = []

    quarter = D // 4
    half = D // 2
    w_start = (2 * group + user) * quarter
    w_core = (2 * group + 1 - user) * quarter
    w_y = (2 * (1 - group) + user) * quarter
    w_diag = (2 * (1 - group) + 1 - user) * quarter
    o_start = user * half
    o_core = (1 - user) * half
    kinds = (
        (w_ref, wb, w_start, quarter),
        (hist_ref.at[0], hb, 0, events),
        (wo_ref, ob, o_start, half),
    )

    barrier = pltpu.get_barrier_semaphore()
    for peer in (ring_peer[0], ring_peer[1], core_peer, y_peer):
        pl.semaphore_signal(barrier, inc=1, device_id=peer, device_id_type=MESH)
    pl.semaphore_wait(barrier, 4)

    def ring_copy(kind, way, step, shard, first):
        source, buffer, start, size = kinds[kind]
        if step == 3:
            size = size // 2
            start = start + way * size
        rows = pl.ds(pl.multiple_of(start, 64), size)
        spot = buffer.at[shard, rows, :]
        return pltpu.make_async_remote_copy(
            src_ref=source.at[rows, :] if first else spot,
            dst_ref=spot,
            send_sem=ring_send.at[kind, way, step],
            recv_sem=ring_recv.at[kind, way, step],
            device_id=ring_peer[way],
            device_id_type=MESH,
        )

    def ring_start(kind, step):
        for way in range(2):
            shard = shard_at(-step if way == 0 else step)
            copy = ring_copy(kind, way, step, shard, step == 0)
            copy.start()
            started.append(copy)

    def ring_wait(kind, step):
        for way in range(2):
            shard = shard_at(-1 - step if way == 0 else step + 1)
            ring_copy(kind, way, step, shard, False).wait_recv()

    def spots(step):
        return ((6, 4),) if step == 3 else ((2 * step, -1 - step), (2 * step + 1, step + 1))

    def side_copy(kind, index, offset):
        buffer, start, size, peer = (
            (wb, w_start, quarter, core_peer),
            (wb, w_start, quarter, y_peer),
            (wb, w_y, quarter, core_peer),
            (ob, o_start, half, core_peer),
        )[kind]
        spot = buffer.at[shard_at(offset), pl.ds(pl.multiple_of(start, 256), size), :]
        return pltpu.make_async_remote_copy(
            src_ref=spot, dst_ref=spot,
            send_sem=side_send.at[kind, index], recv_sem=side_recv.at[kind, index],
            device_id=peer, device_id_type=MESH,
        )

    def side_start(kind, step):
        for index, offset in spots(step):
            copy = side_copy(kind, index, offset)
            copy.start()
            started.append(copy)

    def side_wait(kind, step):
        for index, offset in spots(step):
            buffer, start, size, peer = (
                (wb, w_core, quarter, core_peer),
                (wb, w_y, quarter, y_peer),
                (wb, w_diag, quarter, core_peer),
                (ob, o_core, half, core_peer),
            )[kind]
            spot = buffer.at[shard_at(offset), pl.ds(pl.multiple_of(start, 256), size), :]
            pltpu.make_async_remote_copy(
                src_ref=spot, dst_ref=spot,
                send_sem=side_send.at[kind, index], recv_sem=side_recv.at[kind, index],
                device_id=peer, device_id_type=MESH,
            ).wait_recv()

    W, H, O = 0, 1, 2
    CORE, Y, DIAG, OCORE = 0, 1, 2, 3

    ring_start(W, 0)
    ring_start(H, 0)
    own = [
        pltpu.make_async_copy(w_ref, wb.at[me], local_sem.at[0]),
        pltpu.make_async_copy(hist_ref.at[0], hb.at[me], local_sem.at[1]),
        pltpu.make_async_copy(wo_ref, ob.at[me], local_sem.at[2]),
    ]
    for copy in own:
        copy.start()
    nb[...] = layer_norm(cand_ref[0].astype(jnp.float32)).astype(jnp.bfloat16)
    for copy in own:
        copy.wait()

    def project_cand(shard):
        product = jnp.dot(nb[...], wb[shard], preferred_element_type=jnp.float32)
        act = half_silu(0.5 * product).astype(jnp.bfloat16)
        for i in range(4):
            pb[4 * shard + i] = act[:, i * DH : (i + 1) * DH]

    def project_pair(step):
        @pl.loop(0, 2)
        def _(way):
            project_cand(shard_at((1 - 2 * way) * (step + 1)))

    def spread_rows(step):
        ring_wait(W, step)
        if step < 3:
            ring_start(W, step + 1)
        side_start(Y, step)
        side_start(CORE, step)
        ring_wait(H, step)
        if step < 3:
            ring_start(H, step + 1)

    def spread_out(step):
        ring_wait(O, step)
        if step < 3:
            ring_start(O, step + 1)
        side_start(OCORE, step)

    def gather_rows(step):
        side_wait(Y, step)
        side_start(DIAG, step)
        side_wait(CORE, step)
        side_wait(DIAG, step)

    chunk = 128
    block = 1024
    length = length_ref[0]

    def project_hist(shard):
        @pl.when((shard % 4) // 2 == 1)
        def _():
            first = 4 * shard - 8 - 8 * (shard // 4)

            @pl.loop(0, events // block)
            def _(i):
                start = pl.multiple_of(i * block, block)
                rows = pl.ds(start, block)
                product = jnp.dot(hn[rows, :], wb[shard], preferred_element_type=jnp.float32)
                act = half_silu(0.5 * product)
                event = lax.broadcasted_iota(jnp.int32, act.shape, 0) + start
                act = jnp.where(event < length, act, 0.0).astype(jnp.bfloat16)
                for j in range(4):
                    kvb[first + j, rows, :] = act[:, j * DH : (j + 1) * DH]

    half_scale = 0.5 / math.sqrt(DH)

    def attend(first):
        @pl.loop(0, HEADS // 2, unroll=2)
        def _(i):
            head = first + i
            query = pb[2 * HEADS + head]
            scores = lax.dot_general(
                query, kvb[HEADS + head], (((1,), (1,)), ((), ())),
                preferred_element_type=jnp.float32,
            )
            weights = half_silu(scores * half_scale).astype(jnp.bfloat16)
            mixed = jnp.dot(weights, kvb[head], preferred_element_type=jnp.float32)
            own_sum = jnp.sum(
                query.astype(jnp.float32) * pb[3 * HEADS + head].astype(jnp.float32),
                axis=-1, keepdims=True,
            )
            own_weight = half_silu(own_sum * half_scale)
            ab[head] = mixed + own_weight * pb[HEADS + head].astype(jnp.float32)

    project_cand(me)
    spread_rows(0)
    spread_rows(1)
    ring_start(O, 0)
    gather_rows(0)
    project_pair(0)
    spread_rows(2)
    spread_out(0)
    gather_rows(1)
    project_pair(1)
    spread_rows(3)
    spread_out(1)
    @pl.loop(0, events // chunk)
    def _(i):
        rows = pl.ds(pl.multiple_of(i * chunk, chunk), chunk)
        whole = jnp.concatenate([hb[c, rows, :] for c in range(RING)], axis=1)
        hn[rows, :] = layer_norm(whole.astype(jnp.float32)).astype(jnp.bfloat16)

    gather_rows(2)

    @pl.loop(-1, 2)
    def _(offset):
        project_hist(shard_at(offset))

    spread_out(2)

    @pl.loop(0, 2)
    def _(i):
        project_hist(shard_at(2 - 4 * i))

    project_pair(2)
    spread_out(3)
    side_wait(Y, 3)
    side_start(DIAG, 3)

    @pl.loop(0, 2)
    def _(i):
        project_hist(shard_at(3 - 6 * i))

    near = (HEADS // 2) * (me % 2)
    attend(near)
    side_wait(CORE, 3)
    side_wait(DIAG, 3)
    project_cand(shard_at(4))
    project_hist(shard_at(4))
    attend(HEADS // 2 - near)

    for step in range(4):
        side_wait(OCORE, step)

    @pl.loop(0, slots // chunk)
    def _(i):
        start = pl.multiple_of(i * chunk, chunk)
        rows = pl.ds(start, chunk)
        attn = jnp.concatenate([ab[h, rows, :] for h in range(HEADS)], axis=1)
        gate = jnp.concatenate([pb[h, rows, :] for h in range(HEADS)], axis=1)
        gb[rows, :] = (layer_norm(attn) * gain_ref[...] * gate.astype(jnp.float32)).astype(
            jnp.bfloat16
        )

    for j in range(4):
        columns = pl.ds(j * 256, 256)
        pair = jnp.concatenate([ob[2 * j], ob[2 * j + 1]], axis=1)
        added = jnp.dot(gb[...], pair, preferred_element_type=jnp.float32)
        result = cand_ref[0, :, columns].astype(jnp.float32) + added
        out_ref[0, :, columns] = result.astype(jnp.bfloat16)

    for copy in started:
        copy.wait_send()


def fused_shards(history, hist_len, tile_counts, cand_emb, w_in, out_gain, w_out):
    slots = cand_emb.shape[1]
    events = history.shape[1]
    blocks = 4 * D // DH
    anywhere = pl.BlockSpec(memory_space=pl.ANY)
    vmem = pl.BlockSpec(memory_space=pltpu.VMEM)
    smem = pl.BlockSpec(memory_space=pltpu.SMEM)
    scored = pl.pallas_call(
        fused_kernel,
        out_shape=jax.ShapeDtypeStruct(cand_emb.shape, jnp.bfloat16),
        in_specs=[smem, anywhere, anywhere, anywhere, vmem, vmem],
        out_specs=vmem,
        scratch_shapes=[
            pltpu.VMEM((RING, events, D // RING), jnp.bfloat16),
            pltpu.VMEM((RING, D, 4 * D // RING), jnp.bfloat16),
            pltpu.VMEM((RING, D, D // RING), jnp.bfloat16),
            pltpu.VMEM((slots, D), jnp.bfloat16),
            pltpu.VMEM((events, D), jnp.bfloat16),
            pltpu.VMEM((blocks, slots, DH), jnp.bfloat16),
            pltpu.VMEM((blocks // 2, events, DH), jnp.bfloat16),
            pltpu.VMEM((HEADS, slots, DH), jnp.float32),
            pltpu.VMEM((slots, D), jnp.bfloat16),
            pltpu.SemaphoreType.DMA((3, 2, 4)),
            pltpu.SemaphoreType.DMA((3, 2, 4)),
            pltpu.SemaphoreType.DMA((4, 7)),
            pltpu.SemaphoreType.DMA((4, 7)),
            pltpu.SemaphoreType.DMA((3,)),
        ],
        compiler_params=pltpu.CompilerParams(
            collective_id=0, has_side_effects=True, vmem_limit_bytes=56 * 1024 * 1024
        ),
        name="score_fused",
    )(hist_len, history, w_in, w_out, cand_emb, out_gain.reshape(1, D))
    live = jnp.arange(slots, dtype=jnp.int32) < tile_counts[0, 0] * TILE
    return jnp.where(live[None, :, None], scored, jnp.zeros_like(scored))


def attend_rows(carry, kv_piece, queries, length, score_scale):
    key_count = kv_piece.shape[0]
    values = kv_piece[:, :D].reshape(key_count, HEADS, DH)
    key_heads = kv_piece[:, D:].reshape(key_count, HEADS, DH)
    scores = (
        jnp.einsum("rhe,the->hrt", queries, key_heads, preferred_element_type=jnp.float32)
        * score_scale
    )
    positions = jnp.arange(key_count, dtype=jnp.int32)
    weights = jnp.where(positions[None, None, :] < length, jax.nn.silu(scores), 0.0).astype(
        jnp.bfloat16
    )
    mixed_sum = jnp.einsum("hrt,the->rhe", weights, values, preferred_element_type=jnp.float32)
    return mixed_sum.reshape(carry.shape)


def score_rows(embedded, history, length, w_in, out_gain, w_out):
    score_scale = 1.0 / math.sqrt(DH)
    rows_here = embedded.shape[0]
    normed = layer_norm(embedded.astype(jnp.float32)).astype(jnp.bfloat16)
    initial = jnp.zeros((rows_here, D), jnp.float32)
    own_events = lax.all_to_all(history, "cand", split_axis=0, concat_axis=1, tiled=True)
    hist_normed = layer_norm(own_events.astype(jnp.float32)).astype(jnp.bfloat16)
    stacked = jnp.concatenate([normed, hist_normed], axis=0)
    projected = jax.nn.silu(
        jnp.dot(
            stacked,
            lax.all_gather(w_in, "cand", axis=1, tiled=True),
            preferred_element_type=jnp.float32,
        )
    ).astype(jnp.bfloat16)
    proj_rows = projected[:rows_here]
    hist_proj = projected[rows_here:]
    kv_local = jnp.concatenate([hist_proj[:, D : 2 * D], hist_proj[:, 3 * D :]], axis=1)
    queries = proj_rows[:, 2 * D : 3 * D].reshape(rows_here, HEADS, DH)
    summed = attend_rows(
        initial, lax.all_gather(kv_local, "cand", axis=0, tiled=True), queries, length, score_scale
    )
    gate_part = proj_rows[:, :D].astype(jnp.float32)
    cand_values = proj_rows[:, D : 2 * D].reshape(rows_here, HEADS, DH).astype(jnp.float32)
    cand_keys = proj_rows[:, 3 * D :].reshape(rows_here, HEADS, DH).astype(jnp.float32)
    own_score = jax.nn.silu(jnp.sum(queries.astype(jnp.float32) * cand_keys, axis=-1) * score_scale)
    attn = summed + (own_score[:, :, None] * cand_values).reshape(rows_here, D)
    gated = (layer_norm(attn) * out_gain[None, :] * gate_part).astype(jnp.bfloat16)
    residual = embedded.astype(jnp.float32)
    return (
        residual
        + jnp.dot(
            gated,
            lax.all_gather(w_out, "cand", axis=1, tiled=True),
            preferred_element_type=jnp.float32,
        )
    ).astype(jnp.bfloat16)


def shards(history, hist_len, tile_counts, cand_emb, w_in, out_gain, w_out):
    tile_total = tile_counts[0, 0]
    length = hist_len[0]
    slot_rows = cand_emb[0]
    slot_count = slot_rows.shape[0]
    own_history = history[0]
    scored = score_rows(slot_rows, own_history, length, w_in, out_gain, w_out)
    live = jnp.arange(slot_count, dtype=jnp.int32) < tile_total * TILE
    result = jnp.where(live[:, None], scored, jnp.zeros_like(scored))
    return result[None]


def solution(mesh):
    in_specs = (
        P(("group", "user"), None, "cand"),
        P(("group", "user")),
        P(("group", "user"), "cand"),
        P(("group", "user"), "cand", None),
        P(None, "cand"),
        P(),
        P(None, "cand"),
    )
    out_specs = P(("group", "user"), "cand", None)
    sizes = tuple(mesh.shape[name] for name in ("group", "user", "cand"))
    body = fused_shards if sizes == (2, 2, RING) else shards
    return jax.shard_map(body, mesh=mesh, in_specs=in_specs, out_specs=out_specs, check_vma=False)
```

```python
import functools
import math

import jax
import jax.numpy as jnp
from jax import lax
from jax.experimental import pallas as pl
from jax.experimental.pallas import tpu as pltpu
from jax.sharding import PartitionSpec as P

D = 1024
HEADS = 8
DH = 128
TILE = 128
RING = 8
MESH = pl.DeviceIdType.MESH


def layer_norm(values):
    center = values - jnp.mean(values, axis=-1, keepdims=True)
    spread = jnp.mean(center * center, axis=-1, keepdims=True)
    return center * lax.rsqrt(spread + 1e-05)


def half_silu(half):
    return half + half * jnp.tanh(half)


def cand_of(place):
    high = place // 4
    return (1 - high) * (2 * place) + high * (15 - 2 * place)


def place_of(cand):
    row, column = cand // 2, cand % 2
    return (1 - column) * row + column * (7 - row)


def fused_kernel(
    length_ref, hist_ref, w_ref, wo_ref, cand_ref, gain_ref, out_ref,
    hb, wb, ob, nb, hn, pb, kvb, ab, gb,
    ring_send, ring_recv, side_send, side_recv, local_sem,
):
    group = lax.axis_index("group")
    user = lax.axis_index("user")
    me = lax.axis_index("cand")
    place = place_of(me)
    slots = cand_ref.shape[1]
    events = hist_ref.shape[1]

    def shard_at(offset):
        return cand_of((place + offset + RING) % RING)

    core_peer = {"user": 1 - user}
    y_peer = {"group": 1 - group}
    ring_peer = ({"cand": shard_at(1)}, {"cand": shard_at(-1)})
    started = []

    quarter = D // 4
    half = D // 2
    w_start = (2 * group + user) * quarter
    w_core = (2 * group + 1 - user) * quarter
    w_y = (2 * (1 - group) + user) * quarter
    w_diag = (2 * (1 - group) + 1 - user) * quarter
    o_start = user * half
    o_core = (1 - user) * half
    kinds = (
        (w_ref, wb, w_start, quarter),
        (hist_ref.at[0], hb, 0, events),
        (wo_ref, ob, o_start, half),
    )

    barrier = pltpu.get_barrier_semaphore()
    for peer in (ring_peer[0], ring_peer[1], core_peer, y_peer):
        pl.semaphore_signal(barrier, inc=1, device_id=peer, device_id_type=MESH)
    pl.semaphore_wait(barrier, 4)

    def ring_copy(kind, way, step, shard, first):
        source, buffer, start, size = kinds[kind]
        if step == 3:
            size = size // 2
            start = start + way * size
        rows = pl.ds(pl.multiple_of(start, 64), size)
        spot = buffer.at[shard, rows, :]
        return pltpu.make_async_remote_copy(
            src_ref=source.at[rows, :] if first else spot,
            dst_ref=spot,
            send_sem=ring_send.at[kind, way, step],
            recv_sem=ring_recv.at[kind, way, step],
            device_id=ring_peer[way],
            device_id_type=MESH,
        )

    def ring_start(kind, step):
        for way in range(2):
            shard = shard_at(-step if way == 0 else step)
            copy = ring_copy(kind, way, step, shard, step == 0)
            copy.start()
            started.append(copy)

    def ring_wait(kind, step):
        for way in range(2):
            shard = shard_at(-1 - step if way == 0 else step + 1)
            ring_copy(kind, way, step, shard, False).wait_recv()

    def spots(step):
        return ((6, 4),) if step == 3 else ((2 * step, -1 - step), (2 * step + 1, step + 1))

    def side_copy(kind, index, offset):
        buffer, start, size, peer = (
            (wb, w_start, quarter, core_peer),
            (wb, w_start, quarter, y_peer),
            (wb, w_y, quarter, core_peer),
            (ob, o_start, half, core_peer),
        )[kind]
        spot = buffer.at[shard_at(offset), pl.ds(pl.multiple_of(start, 256), size), :]
        return pltpu.make_async_remote_copy(
            src_ref=spot, dst_ref=spot,
            send_sem=side_send.at[kind, index], recv_sem=side_recv.at[kind, index],
            device_id=peer, device_id_type=MESH,
        )

    def side_start(kind, step):
        for index, offset in spots(step):
            copy = side_copy(kind, index, offset)
            copy.start()
            started.append(copy)

    def side_wait(kind, step):
        for index, offset in spots(step):
            buffer, start, size, peer = (
                (wb, w_core, quarter, core_peer),
                (wb, w_y, quarter, y_peer),
                (wb, w_diag, quarter, core_peer),
                (ob, o_core, half, core_peer),
            )[kind]
            spot = buffer.at[shard_at(offset), pl.ds(pl.multiple_of(start, 256), size), :]
            pltpu.make_async_remote_copy(
                src_ref=spot, dst_ref=spot,
                send_sem=side_send.at[kind, index], recv_sem=side_recv.at[kind, index],
                device_id=peer, device_id_type=MESH,
            ).wait_recv()

    W, H, O = 0, 1, 2
    CORE, Y, DIAG, OCORE = 0, 1, 2, 3

    ring_start(W, 0)
    ring_start(H, 0)
    own = [
        pltpu.make_async_copy(w_ref, wb.at[me], local_sem.at[0]),
        pltpu.make_async_copy(hist_ref.at[0], hb.at[me], local_sem.at[1]),
        pltpu.make_async_copy(wo_ref, ob.at[me], local_sem.at[2]),
    ]
    for copy in own:
        copy.start()
    nb[...] = layer_norm(cand_ref[0].astype(jnp.float32)).astype(jnp.bfloat16)
    for copy in own:
        copy.wait()

    def project_cand(shard):
        product = jnp.dot(nb[...], wb[shard], preferred_element_type=jnp.float32)
        act = half_silu(0.5 * product).astype(jnp.bfloat16)
        for i in range(4):
            pb[4 * shard + i] = act[:, i * DH : (i + 1) * DH]

    def project_pair(step):
        @pl.loop(0, 2)
        def _(way):
            project_cand(shard_at((1 - 2 * way) * (step + 1)))

    def spread_rows(step):
        ring_wait(W, step)
        if step < 3:
            ring_start(W, step + 1)
        side_start(Y, step)
        side_start(CORE, step)
        ring_wait(H, step)
        if step < 3:
            ring_start(H, step + 1)

    def spread_out(step):
        ring_wait(O, step)
        if step < 3:
            ring_start(O, step + 1)
        side_start(OCORE, step)

    def gather_rows(step):
        side_wait(Y, step)
        side_start(DIAG, step)
        side_wait(CORE, step)
        side_wait(DIAG, step)

    chunk = 128
    block = 1024
    length = length_ref[0]

    def project_hist(shard):
        @pl.when((shard % 4) // 2 == 1)
        def _():
            first = 4 * shard - 8 - 8 * (shard // 4)

            @pl.loop(0, events // block)
            def _(i):
                start = pl.multiple_of(i * block, block)
                rows = pl.ds(start, block)
                product = jnp.dot(hn[rows, :], wb[shard], preferred_element_type=jnp.float32)
                act = half_silu(0.5 * product)
                event = lax.broadcasted_iota(jnp.int32, act.shape, 0) + start
                act = jnp.where(event < length, act, 0.0).astype(jnp.bfloat16)
                for j in range(4):
                    kvb[first + j, rows, :] = act[:, j * DH : (j + 1) * DH]

    half_scale = 0.5 / math.sqrt(DH)

    def attend(first):
        @pl.loop(0, HEADS // 2, unroll=4)
        def _(i):
            head = first + i
            query = pb[2 * HEADS + head]
            scores = lax.dot_general(
                query, kvb[HEADS + head], (((1,), (1,)), ((), ())),
                preferred_element_type=jnp.float32,
            )
            weights = half_silu(scores * half_scale).astype(jnp.bfloat16)
            mixed = jnp.dot(weights, kvb[head], preferred_element_type=jnp.float32)
            own_sum = jnp.sum(
                query.astype(jnp.float32) * pb[3 * HEADS + head].astype(jnp.float32),
                axis=-1, keepdims=True,
            )
            own_weight = half_silu(own_sum * half_scale)
            ab[head] = mixed + own_weight * pb[HEADS + head].astype(jnp.float32)

    project_cand(me)
    spread_rows(0)
    spread_rows(1)
    ring_start(O, 0)
    gather_rows(0)
    project_pair(0)
    spread_rows(2)
    spread_out(0)
    gather_rows(1)
    project_pair(1)
    spread_rows(3)
    spread_out(1)
    @pl.loop(0, events // chunk)
    def _(i):
        rows = pl.ds(pl.multiple_of(i * chunk, chunk), chunk)
        whole = jnp.concatenate([hb[c, rows, :] for c in range(RING)], axis=1)
        hn[rows, :] = layer_norm(whole.astype(jnp.float32)).astype(jnp.bfloat16)

    gather_rows(2)

    @pl.loop(-1, 2)
    def _(offset):
        project_hist(shard_at(offset))

    spread_out(2)

    @pl.loop(0, 2)
    def _(i):
        project_hist(shard_at(2 - 4 * i))

    project_pair(2)
    spread_out(3)
    side_wait(Y, 3)
    side_start(DIAG, 3)

    @pl.loop(0, 2)
    def _(i):
        project_hist(shard_at(3 - 6 * i))

    near = (HEADS // 2) * (me % 2)
    attend(near)
    side_wait(CORE, 3)
    side_wait(DIAG, 3)
    project_cand(shard_at(4))
    project_hist(shard_at(4))
    attend(HEADS // 2 - near)

    for step in range(4):
        side_wait(OCORE, step)

    @pl.loop(0, slots // chunk)
    def _(i):
        start = pl.multiple_of(i * chunk, chunk)
        rows = pl.ds(start, chunk)
        attn = jnp.concatenate([ab[h, rows, :] for h in range(HEADS)], axis=1)
        gate = jnp.concatenate([pb[h, rows, :] for h in range(HEADS)], axis=1)
        gb[rows, :] = (layer_norm(attn) * gain_ref[...] * gate.astype(jnp.float32)).astype(
            jnp.bfloat16
        )

    for j in range(4):
        columns = pl.ds(j * 256, 256)
        pair = jnp.concatenate([ob[2 * j], ob[2 * j + 1]], axis=1)
        added = jnp.dot(gb[...], pair, preferred_element_type=jnp.float32)
        result = cand_ref[0, :, columns].astype(jnp.float32) + added
        out_ref[0, :, columns] = result.astype(jnp.bfloat16)

    for copy in started:
        copy.wait_send()


def fused_shards(history, hist_len, tile_counts, cand_emb, w_in, out_gain, w_out):
    slots = cand_emb.shape[1]
    events = history.shape[1]
    blocks = 4 * D // DH
    anywhere = pl.BlockSpec(memory_space=pl.ANY)
    vmem = pl.BlockSpec(memory_space=pltpu.VMEM)
    smem = pl.BlockSpec(memory_space=pltpu.SMEM)
    scored = pl.pallas_call(
        fused_kernel,
        out_shape=jax.ShapeDtypeStruct(cand_emb.shape, jnp.bfloat16),
        in_specs=[smem, anywhere, anywhere, anywhere, vmem, vmem],
        out_specs=vmem,
        scratch_shapes=[
            pltpu.VMEM((RING, events, D // RING), jnp.bfloat16),
            pltpu.VMEM((RING, D, 4 * D // RING), jnp.bfloat16),
            pltpu.VMEM((RING, D, D // RING), jnp.bfloat16),
            pltpu.VMEM((slots, D), jnp.bfloat16),
            pltpu.VMEM((events, D), jnp.bfloat16),
            pltpu.VMEM((blocks, slots, DH), jnp.bfloat16),
            pltpu.VMEM((blocks // 2, events, DH), jnp.bfloat16),
            pltpu.VMEM((HEADS, slots, DH), jnp.float32),
            pltpu.VMEM((slots, D), jnp.bfloat16),
            pltpu.SemaphoreType.DMA((3, 2, 4)),
            pltpu.SemaphoreType.DMA((3, 2, 4)),
            pltpu.SemaphoreType.DMA((4, 7)),
            pltpu.SemaphoreType.DMA((4, 7)),
            pltpu.SemaphoreType.DMA((3,)),
        ],
        compiler_params=pltpu.CompilerParams(
            collective_id=0, has_side_effects=True, vmem_limit_bytes=56 * 1024 * 1024
        ),
        name="score_fused",
    )(hist_len, history, w_in, w_out, cand_emb, out_gain.reshape(1, D))
    live = jnp.arange(slots, dtype=jnp.int32) < tile_counts[0, 0] * TILE
    return jnp.where(live[None, :, None], scored, jnp.zeros_like(scored))


def attend_rows(carry, kv_piece, queries, length, score_scale):
    key_count = kv_piece.shape[0]
    values = kv_piece[:, :D].reshape(key_count, HEADS, DH)
    key_heads = kv_piece[:, D:].reshape(key_count, HEADS, DH)
    scores = (
        jnp.einsum("rhe,the->hrt", queries, key_heads, preferred_element_type=jnp.float32)
        * score_scale
    )
    positions = jnp.arange(key_count, dtype=jnp.int32)
    weights = jnp.where(positions[None, None, :] < length, jax.nn.silu(scores), 0.0).astype(
        jnp.bfloat16
    )
    mixed_sum = jnp.einsum("hrt,the->rhe", weights, values, preferred_element_type=jnp.float32)
    return mixed_sum.reshape(carry.shape)


def score_rows(embedded, history, length, w_in, out_gain, w_out):
    score_scale = 1.0 / math.sqrt(DH)
    rows_here = embedded.shape[0]
    normed = layer_norm(embedded.astype(jnp.float32)).astype(jnp.bfloat16)
    initial = jnp.zeros((rows_here, D), jnp.float32)
    own_events = lax.all_to_all(history, "cand", split_axis=0, concat_axis=1, tiled=True)
    hist_normed = layer_norm(own_events.astype(jnp.float32)).astype(jnp.bfloat16)
    stacked = jnp.concatenate([normed, hist_normed], axis=0)
    projected = jax.nn.silu(
        jnp.dot(
            stacked,
            lax.all_gather(w_in, "cand", axis=1, tiled=True),
            preferred_element_type=jnp.float32,
        )
    ).astype(jnp.bfloat16)
    proj_rows = projected[:rows_here]
    hist_proj = projected[rows_here:]
    kv_local = jnp.concatenate([hist_proj[:, D : 2 * D], hist_proj[:, 3 * D :]], axis=1)
    queries = proj_rows[:, 2 * D : 3 * D].reshape(rows_here, HEADS, DH)
    summed = attend_rows(
        initial, lax.all_gather(kv_local, "cand", axis=0, tiled=True), queries, length, score_scale
    )
    gate_part = proj_rows[:, :D].astype(jnp.float32)
    cand_values = proj_rows[:, D : 2 * D].reshape(rows_here, HEADS, DH).astype(jnp.float32)
    cand_keys = proj_rows[:, 3 * D :].reshape(rows_here, HEADS, DH).astype(jnp.float32)
    own_score = jax.nn.silu(jnp.sum(queries.astype(jnp.float32) * cand_keys, axis=-1) * score_scale)
    attn = summed + (own_score[:, :, None] * cand_values).reshape(rows_here, D)
    gated = (layer_norm(attn) * out_gain[None, :] * gate_part).astype(jnp.bfloat16)
    residual = embedded.astype(jnp.float32)
    return (
        residual
        + jnp.dot(
            gated,
            lax.all_gather(w_out, "cand", axis=1, tiled=True),
            preferred_element_type=jnp.float32,
        )
    ).astype(jnp.bfloat16)


def shards(history, hist_len, tile_counts, cand_emb, w_in, out_gain, w_out):
    tile_total = tile_counts[0, 0]
    length = hist_len[0]
    slot_rows = cand_emb[0]
    slot_count = slot_rows.shape[0]
    own_history = history[0]
    scored = score_rows(slot_rows, own_history, length, w_in, out_gain, w_out)
    live = jnp.arange(slot_count, dtype=jnp.int32) < tile_total * TILE
    result = jnp.where(live[:, None], scored, jnp.zeros_like(scored))
    return result[None]


def solution(mesh):
    in_specs = (
        P(("group", "user"), None, "cand"),
        P(("group", "user")),
        P(("group", "user"), "cand"),
        P(("group", "user"), "cand", None),
        P(None, "cand"),
        P(),
        P(None, "cand"),
    )
    out_specs = P(("group", "user"), "cand", None)
    sizes = tuple(mesh.shape[name] for name in ("group", "user", "cand"))
    body = fused_shards if sizes == (2, 2, RING) else shards
    return jax.shard_map(body, mesh=mesh, in_specs=in_specs, out_specs=out_specs, check_vma=False)
```
